512 devices in a mesh: section: 16 (over y, z_hi), dp: 32 (over z_lo, x, core).
Axes of the slice: x: 4, y: 8, z: 8 (z_hi: 2, z_lo: 4; z = z_hi * 4 + z_lo), core: 2. Of those that a mesh axis runs over, the one named last changes fastest.
Arguments:
- section_input: bfloat16 [6, 768, 3072], P(None, 'dp'), may hold values from -6 to 6
- loss_grad: bfloat16 [6, 768, 3072], P(None, 'dp'), may hold values from -6 to 6
- norm_gain: float32 [16, 3072], P('section'), may hold values from 0.1 to 1.9
- channel_order: int32 [16, 3072], P('section'), may hold values from 0 to 3071, each once within a row
- right_factor: bfloat16 [16, 3072, 768], P('section', 'dp'), may hold values from -0.15625 to 0.15625
- left_factor: bfloat16 [16, 3072, 768], P('section', 'dp'), may hold values from -0.15625 to 0.15625
Outputs:
- section_output: bfloat16 [16, 6, 768, 3072], P('section', None, 'dp')
- left_grad: float32 [16, 768, 768], P('section', 'dp')
The draws below stay inside these ranges and needn't reach their ends.
Inputs may be any that keep to these rules, and one draw needn't show every extreme that they name: `channel_order`: each layer's row is a permutation of the 3072 channels.
All inputs are finite; a program needn't handle non-finite values.
Results may differ from the reference program's by a relative error of at most 0.03.
Values may be sent and summed in bfloat16 or wider, within the bound.
A program may use at most 64 MiB of HBM per device.

```python
import jax
import jax.numpy as jnp
from jax import lax

D = 3072
BLK = 768
MICRO = 6
MB_TOK = 24
TOKENS_MB = 768
LAYERS = 16
N_DP = 32


def block_scale(rng, dims, cuts, smallest, top_value):
    def one(position, parts):
        heights = jax.random.uniform(jax.random.fold_in(jax.random.fold_in(rng, 6), position), (parts,), jnp.float32, smallest / len(cuts), top_value / len(cuts))
        return jnp.repeat(jnp.exp(heights), dims[position] // parts).reshape((-1,) + (1,) * (len(dims) - position - 1))

    gain = one(*cuts[0])
    for cut in cuts[1:]:
        gain = gain * one(*cut)
    return gain


def scatter_about(stream_key, dims, width, most, cuts=(), kind=jnp.bfloat16):
    drawn = jax.random.normal(stream_key, dims, jnp.float32) * width
    if len(cuts) > 0:
        drawn = block_scale(stream_key, dims, cuts, -0.22, 0.18) * drawn
    return jnp.clip(drawn, min=-most, max=most).astype(kind)


def setup_inputs(seed: int = 0) -> dict:
    seeds = jax.random.split(jax.random.key(seed), 7)
    return {
        "section_input": scatter_about(seeds[0], (MICRO, TOKENS_MB, D), 1.0, 6.0, ((1, 32),)),
        "loss_grad": scatter_about(seeds[1], (MICRO, TOKENS_MB, D), 1.0, 6.0, ((1, 32),)),
        "norm_gain": jnp.clip(1.0 + 0.18 * jax.random.normal(seeds[2], (LAYERS, D), jnp.float32), 0.1, 1.9),
        "channel_order": jax.vmap(lambda own: jax.random.permutation(own, D))(jax.random.split(seeds[3], LAYERS)).reshape((LAYERS, D)).astype(jnp.int32),
        "right_factor": scatter_about(seeds[4], (LAYERS, D, BLK), (2 * BLK) ** -0.5, 0.15625, ((0, 16), (1, 32))),
        "left_factor": scatter_about(seeds[5], (LAYERS, D, BLK), (2 * BLK) ** -0.5, 0.15625, ((0, 16), (1, 32))),
    }


epsilon = 1e-05

def block_apply(values, factor):
    row_count = values.shape[0]
    block_size = factor.shape[1]
    block_count = factor.shape[0] // block_size
    result = jnp.einsum('rnk,nkj->rnj', values.reshape(row_count, block_count, block_size).astype(jnp.float32), factor.reshape(block_count, block_size, block_size).astype(jnp.float32))
    return result.reshape(row_count, block_count * block_size)

def block_transposed(values, factor):
    row_count = values.shape[0]
    block_size = factor.shape[1]
    block_count = factor.shape[0] // block_size
    result = jnp.einsum('rnj,nkj->rnk', values.reshape(row_count, block_count, block_size).astype(jnp.float32), factor.reshape(block_count, block_size, block_size).astype(jnp.float32))
    return result.reshape(row_count, block_count * block_size)

def inverse_norm(inputs):
    wide_in = inputs.astype(jnp.float32)
    return (wide_in, lax.rsqrt(lax.optimization_barrier(jnp.mean(wide_in * wide_in, axis=-1, keepdims=True)) + epsilon))

def layer_forward(inputs, gain_row, shuffle, right_full, left_full):
    wide_in, inverse_rms = inverse_norm(inputs)
    normed = (wide_in * inverse_rms * gain_row).astype(jnp.bfloat16)
    mixed = block_apply(normed, right_full).astype(jnp.bfloat16)
    permuted = jnp.take(mixed, shuffle, axis=1)
    output = (wide_in + block_apply(permuted, left_full)).astype(jnp.bfloat16)
    return (output, permuted)

def layer_backward(inputs, upstream, gain_row, inverse, right_full, left_full):
    wide_in, inverse_rms = inverse_norm(inputs)
    through = block_transposed(upstream, left_full).astype(jnp.bfloat16)
    before = jnp.take(through, inverse, axis=1)
    scaled = block_transposed(before, right_full) * gain_row
    cubed = inverse_rms * inverse_rms * inverse_rms
    grad_input = upstream.astype(jnp.float32) + inverse_rms * scaled - wide_in * cubed * lax.optimization_barrier(jnp.mean(scaled * wide_in, axis=-1, keepdims=True))
    return grad_input.astype(jnp.bfloat16)

def device_sums(left_rows, right_rows):
    shaped_left = left_rows[:, :BLK].reshape(MICRO, N_DP, MB_TOK, BLK).astype(jnp.float32)
    shaped_right = right_rows[:, :BLK].reshape(MICRO, N_DP, MB_TOK, BLK).astype(jnp.float32)
    terms = jnp.einsum('mdrk,mdrj->dkj', shaped_left, shaped_right)
    rounded = lax.optimization_barrier(terms.astype(jnp.bfloat16))
    return lax.optimization_barrier(jnp.sum(rounded.astype(jnp.float32), axis=0))

def reference(section_input, loss_grad, norm_gain, channel_order, right_factor, left_factor):
    hidden = section_input.reshape(-1, D)
    saved_inputs = []
    saved_permuted = []
    outputs = []
    for layer_num in range(LAYERS):
        saved_inputs.append(hidden)
        hidden, permuted = layer_forward(hidden, norm_gain[layer_num], channel_order[layer_num], right_factor[layer_num], left_factor[layer_num])
        saved_permuted.append(permuted)
        outputs.append(hidden.reshape(MICRO, TOKENS_MB, D))
    upstream = loss_grad.reshape(-1, D)
    left_list = [None] * LAYERS
    for layer_num in reversed(range(LAYERS)):
        shuffle = channel_order[layer_num]
        inverse = jnp.zeros((D,), jnp.int32).at[shuffle].set(jnp.arange(D, dtype=jnp.int32))
        grad_input = layer_backward(saved_inputs[layer_num], upstream, norm_gain[layer_num], inverse, right_factor[layer_num], left_factor[layer_num])
        left_list[layer_num] = device_sums(saved_permuted[layer_num], upstream)
        upstream = grad_input
    return (jnp.stack(outputs), jnp.stack(left_list))
```

```python
import jax
import jax.numpy as jnp
from jax import lax
from jax.experimental import pallas as pl
from jax.sharding import PartitionSpec as P

epsilon = 1e-05


def shifted(array, axis, by):
    peers = lax.axis_size(axis)
    pairs = [(i, i + by) for i in range(peers) if 0 <= i + by < peers]
    return lax.ppermute(array, axis, pairs)


def whole_kernel(right_ref, rows_ref, owner_ref, gain_ref, whole_ref):
    column_block = pl.program_id(1)
    spread = jnp.where(
        owner_ref[...] == column_block, rows_ref[...].astype(jnp.float32), 0.0
    ).astype(jnp.bfloat16)
    product = jnp.dot(right_ref[...], spread, preferred_element_type=jnp.float32)
    whole_ref[...] = (product * gain_ref[...]).astype(jnp.bfloat16)


def build_maps(gain_row, order, right_full, left_full):
    channels, block = left_full.shape
    count = channels // block
    inverse = jnp.zeros((channels,), jnp.int32).at[order].set(jnp.arange(channels, dtype=jnp.int32))
    rows = jnp.take(left_full, inverse, axis=0)
    whole = pl.pallas_call(
        whole_kernel,
        grid=(count, count),
        in_specs=[
            pl.BlockSpec((block, block), lambda n, b: (n, 0)),
            pl.BlockSpec((block, block), lambda n, b: (n, 0)),
            pl.BlockSpec((block, 1), lambda n, b: (n, 0)),
            pl.BlockSpec((block, 1), lambda n, b: (n, 0)),
        ],
        out_specs=pl.BlockSpec((block, block), lambda n, b: (n, b)),
        out_shape=jax.ShapeDtypeStruct((channels, channels), jnp.bfloat16),
        name="whole_map",
    )(right_full, rows, (inverse // block)[:, None], gain_row[:, None])
    pick = (order[None, :block] == jnp.arange(channels)[:, None]).astype(jnp.bfloat16)
    head = jnp.einsum(
        "nkj,nji->nki",
        right_full.reshape(count, block, block),
        pick.reshape(count, block, block),
        preferred_element_type=jnp.float32,
    ).astype(jnp.bfloat16).reshape(channels, block)
    return whole, head


def inverse_norm(wide_in):
    return lax.rsqrt(jnp.mean(wide_in * wide_in, axis=-1, keepdims=True) + epsilon)


def per_device(section_input, loss_grad, norm_gain, channel_order, right_factor, left_factor):
    sections = lax.axis_size("section")
    section_index = lax.axis_index("section")
    micro_count, row_count, channels = section_input.shape
    block_size = right_factor.shape[2]
    left_full = lax.all_gather(left_factor[0], "dp", axis=0, tiled=True)
    right_full = lax.all_gather(right_factor[0], "dp", axis=0, tiled=True)
    gain_row = norm_gain[0]
    whole, head = build_maps(gain_row, channel_order[0], right_full, left_full)
    is_first = section_index == 0
    is_last = section_index == sections - 1
    empty_rows = jnp.zeros((row_count, channels), jnp.bfloat16)
    empty_buf = jnp.zeros((micro_count + 1, row_count, channels), jnp.bfloat16)

    def slots(batch_pos):
        is_valid = (batch_pos >= 0) & (batch_pos < micro_count)
        return jnp.clip(batch_pos, 0, micro_count - 1), jnp.where(is_valid, batch_pos, micro_count)

    def forward_step(state, step_num):
        incoming, saved_in, outputs = state
        read, write = slots(step_num - section_index)
        inputs = jnp.where(
            is_first, lax.dynamic_index_in_dim(section_input, read, 0, keepdims=False), incoming
        )
        wide_in = inputs.astype(jnp.float32)
        product = jnp.dot(inputs, whole, preferred_element_type=jnp.float32)
        output = (wide_in + inverse_norm(wide_in) * product).astype(jnp.bfloat16)
        passed = shifted(output, "section", 1)
        saved_in = lax.dynamic_update_index_in_dim(saved_in, inputs, write, 0)
        outputs = lax.dynamic_update_index_in_dim(outputs, output, write, 0)
        return (passed, saved_in, outputs), None

    steps = jnp.arange(sections + micro_count - 1, dtype=jnp.int32)
    (_, saved_in, outputs), _ = lax.scan(forward_step, (empty_rows, empty_buf, empty_buf), steps)

    def backward_step(state, step_num):
        incoming, saved_up = state
        read, write = slots(step_num - (sections - 1) + section_index)
        upstream = jnp.where(
            is_last, lax.dynamic_index_in_dim(loss_grad, read, 0, keepdims=False), incoming
        )
        wide_in = lax.dynamic_index_in_dim(saved_in, read, 0, keepdims=False).astype(jnp.float32)
        inverse_rms = inverse_norm(wide_in)
        scaled = lax.dot_general(
            upstream, whole, (((1,), (1,)), ((), ())), preferred_element_type=jnp.float32
        )
        grad_input = (
            upstream.astype(jnp.float32)
            + inverse_rms * scaled
            - wide_in * (inverse_rms * inverse_rms * inverse_rms)
            * jnp.mean(scaled * wide_in, axis=-1, keepdims=True)
        ).astype(jnp.bfloat16)
        passed = shifted(grad_input, "section", -1)
        saved_up = lax.dynamic_update_index_in_dim(saved_up, upstream[:, :block_size], write, 0)
        return (passed, saved_up), None

    empty_head = jnp.zeros((micro_count + 1, row_count, block_size), jnp.bfloat16)
    (_, saved_up), _ = lax.scan(backward_step, (empty_rows, empty_head), steps)

    row_total = micro_count * row_count
    wide_in = saved_in[:micro_count].reshape(row_total, channels).astype(jnp.float32)
    normed = (wide_in * inverse_norm(wide_in) * gain_row).astype(jnp.bfloat16)
    permuted = jnp.dot(normed, head, preferred_element_type=jnp.float32).astype(jnp.bfloat16)
    return (outputs[None, :micro_count], left_gradient(permuted, saved_up[:micro_count].reshape(row_total, block_size))[None])


def left_gradient(left_rows, right_rows):
    peers = lax.axis_size("dp")
    block_size = left_rows.shape[1]
    term = lax.dot_general(
        left_rows, right_rows, (((0,), (0,)), ((), ())), preferred_element_type=jnp.float32
    ).astype(jnp.bfloat16)
    parts = lax.all_to_all(
        term.reshape(peers, block_size // peers, block_size), "dp", split_axis=0, concat_axis=0
    )
    return jnp.sum(parts.astype(jnp.float32), axis=0)


def solution(mesh):
    in_specs = (
        P(None, "dp", None),
        P(None, "dp", None),
        P("section", None),
        P("section", None),
        P("section", "dp", None),
        P("section", "dp", None),
    )
    out_specs = (P("section", None, "dp", None), P("section", "dp", None))
    return jax.shard_map(
        per_device, mesh=mesh, in_specs=in_specs, out_specs=out_specs, check_vma=False
    )
```

```python
import functools

import jax
import jax.numpy as jnp
from jax import lax
from jax.experimental import pallas as pl
from jax.experimental.pallas import tpu as pltpu
from jax.sharding import PartitionSpec as P

epsilon = 1e-05


def whole_kernel(right_ref, rows_ref, owner_ref, gain_ref, whole_ref):
    column_block = pl.program_id(1)
    spread = jnp.where(
        owner_ref[...] == column_block, rows_ref[...].astype(jnp.float32), 0.0
    ).astype(jnp.bfloat16)
    product = jnp.dot(right_ref[...], spread, preferred_element_type=jnp.float32)
    whole_ref[...] = (product * gain_ref[...]).astype(jnp.bfloat16)


def build_maps(gain_row, order, right_full, left_full):
    channels, block = left_full.shape
    count = channels // block
    inverse = jnp.zeros((channels,), jnp.int32).at[order].set(jnp.arange(channels, dtype=jnp.int32))
    rows = jnp.take(left_full, inverse, axis=0)
    whole = pl.pallas_call(
        whole_kernel,
        grid=(count, count),
        in_specs=[
            pl.BlockSpec((block, block), lambda n, b: (n, 0)),
            pl.BlockSpec((block, block), lambda n, b: (n, 0)),
            pl.BlockSpec((block, 1), lambda n, b: (n, 0)),
            pl.BlockSpec((block, 1), lambda n, b: (n, 0)),
        ],
        out_specs=pl.BlockSpec((block, block), lambda n, b: (n, b)),
        out_shape=jax.ShapeDtypeStruct((channels, channels), jnp.bfloat16),
        name="whole_map",
    )(right_full, rows, (inverse // block)[:, None], gain_row[:, None])
    pick = (order[None, :block] == jnp.arange(channels)[:, None]).astype(jnp.bfloat16)
    head = jnp.einsum(
        "nkj,nji->nki",
        right_full.reshape(count, block, block),
        pick.reshape(count, block, block),
        preferred_element_type=jnp.float32,
    ).astype(jnp.bfloat16).reshape(channels, block)
    return whole, head


def inverse_norm(wide_in):
    return lax.rsqrt(jnp.mean(wide_in * wide_in, axis=-1, keepdims=True) + epsilon)


def relay_kernel(
    sections, in_ref, grad_ref, whole_ref, out_ref, saved_ref, up_ref,
    held, upstream, sent, scaled, forward_send, forward_recv, backward_send, backward_recv,
):
    me = lax.axis_index("section")
    micro_count, row_count, channels = held.shape
    chunk = up_ref.shape[2]
    after = lax.rem(me + 1, sections)
    ahead = lax.rem(me + sections - 1, sections)

    barrier = pltpu.get_barrier_semaphore()
    for neighbour in (after, ahead):
        pl.semaphore_signal(
            barrier, inc=1, device_id={"section": neighbour}, device_id_type=pl.DeviceIdType.MESH
        )

    @pl.when(me == 0)
    def first_inputs():
        held[...] = in_ref[...]

    @pl.when(me == sections - 1)
    def last_grads():
        upstream[...] = grad_ref[...]

    pl.semaphore_wait(barrier, 2)

    def forward_copy(slot):
        return pltpu.make_async_remote_copy(
            src_ref=out_ref.at[slot],
            dst_ref=held.at[slot],
            send_sem=forward_send.at[slot],
            recv_sem=forward_recv.at[slot],
            device_id={"section": after},
            device_id_type=pl.DeviceIdType.MESH,
        )

    def backward_copy(slot):
        return pltpu.make_async_remote_copy(
            src_ref=sent.at[slot],
            dst_ref=upstream.at[slot],
            send_sem=backward_send.at[slot],
            recv_sem=backward_recv.at[slot],
            device_id={"section": ahead},
            device_id_type=pl.DeviceIdType.MESH,
        )

    def run_forward(slot):
        @pl.when(me > 0)
        def arrived():
            forward_copy(slot).wait_recv()

        wide = held[slot].astype(jnp.float32)
        inverse_rms = inverse_norm(wide)

        def columns(part, carry):
            cols = pl.ds(pl.multiple_of(part * chunk, chunk), chunk)
            product = jnp.dot(held[slot], whole_ref[:, cols], preferred_element_type=jnp.float32)
            out_ref[slot, :, cols] = (
                held[slot, :, cols].astype(jnp.float32) + inverse_rms * product
            ).astype(jnp.bfloat16)
            return carry

        lax.fori_loop(0, channels // chunk, columns, 0)

        @pl.when(me < sections - 1)
        def pass_on():
            forward_copy(slot).start()

    def run_backward(slot):
        @pl.when(me < sections - 1)
        def arrived():
            backward_copy(slot).wait_recv()

        @pl.when(me > 0)
        def compute():
            def columns(part, carry):
                cols = pl.ds(pl.multiple_of(part * chunk, chunk), chunk)
                scaled[:, cols] = lax.dot_general(
                    upstream[slot], whole_ref[cols, :], (((1,), (1,)), ((), ())),
                    preferred_element_type=jnp.float32,
                )
                return carry

            lax.fori_loop(0, channels // chunk, columns, 0)
            wide = held[slot].astype(jnp.float32)
            inverse_rms = inverse_norm(wide)
            terms = scaled[...]
            along = jnp.mean(terms * wide, axis=-1, keepdims=True)
            cubed = inverse_rms * inverse_rms * inverse_rms
            sent[slot] = (
                upstream[slot].astype(jnp.float32) + inverse_rms * terms - wide * (cubed * along)
            ).astype(jnp.bfloat16)
            backward_copy(slot).start()

    def tick(step, carry):
        forward_slot = step - me
        backward_slot = step - (2 * sections - 1) + me

        @pl.when((forward_slot >= 0) & (forward_slot < micro_count))
        def forward_part():
            run_forward(forward_slot)

        @pl.when((backward_slot >= 0) & (backward_slot < micro_count))
        def backward_part():
            run_backward(backward_slot)

        return carry

    lax.fori_loop(0, 2 * sections - 1 + micro_count, tick, 0)
    saved_ref[...] = held[...]
    up_ref[...] = upstream[:, :, :chunk]

    @pl.when(me < sections - 1)
    def forward_sent():
        for slot in range(micro_count):
            forward_copy(slot).wait_send()

    @pl.when(me > 0)
    def backward_sent():
        for slot in range(micro_count):
            backward_copy(slot).wait_send()


def relay(sections, section_input, loss_grad, whole, block_size):
    shape = section_input.shape
    head_shape = shape[:2] + (block_size,)
    vmem = pl.BlockSpec(memory_space=pltpu.VMEM)
    sems = pltpu.SemaphoreType.DMA((shape[0],))
    return pl.pallas_call(
        functools.partial(relay_kernel, sections),
        out_shape=[
            jax.ShapeDtypeStruct(shape, jnp.bfloat16),
            jax.ShapeDtypeStruct(shape, jnp.bfloat16),
            jax.ShapeDtypeStruct(head_shape, jnp.bfloat16),
        ],
        in_specs=[vmem] * 3,
        out_specs=[vmem] * 3,
        scratch_shapes=[
            pltpu.VMEM(shape, jnp.bfloat16),
            pltpu.VMEM(shape, jnp.bfloat16),
            pltpu.VMEM(shape, jnp.bfloat16),
            pltpu.VMEM(shape[1:], jnp.float32),
            sems, sems, sems, sems,
        ],
        compiler_params=pltpu.CompilerParams(
            collective_id=0, has_side_effects=True, vmem_limit_bytes=48 * 1024 * 1024
        ),
        name="relay",
    )(section_input, loss_grad, whole)


def per_device(section_input, loss_grad, norm_gain, channel_order, right_factor, left_factor):
    sections = lax.axis_size("section")
    micro_count, row_count, channels = section_input.shape
    block_size = right_factor.shape[2]
    left_full = lax.all_gather(left_factor[0], "dp", axis=0, tiled=True)
    right_full = lax.all_gather(right_factor[0], "dp", axis=0, tiled=True)
    gain_row = norm_gain[0]
    whole, head = build_maps(gain_row, channel_order[0], right_full, left_full)
    outputs, saved_in, saved_up = relay(sections, section_input, loss_grad, whole, block_size)

    row_total = micro_count * row_count
    wide_in = saved_in.reshape(row_total, channels).astype(jnp.float32)
    normed = (wide_in * inverse_norm(wide_in) * gain_row).astype(jnp.bfloat16)
    permuted = jnp.dot(normed, head, preferred_element_type=jnp.float32).astype(jnp.bfloat16)
    left_shard = left_gradient(permuted, saved_up.reshape(row_total, block_size))
    return (outputs[None], left_shard[None])


def left_gradient(left_rows, right_rows):
    peers = lax.axis_size("dp")
    block_size = left_rows.shape[1]
    term = lax.dot_general(
        left_rows, right_rows, (((0,), (0,)), ((), ())), preferred_element_type=jnp.float32
    ).astype(jnp.bfloat16)
    parts = lax.all_to_all(
        term.reshape(peers, block_size // peers, block_size), "dp", split_axis=0, concat_axis=0
    )
    return jnp.sum(parts.astype(jnp.float32), axis=0)


def solution(mesh):
    in_specs = (
        P(None, "dp", None),
        P(None, "dp", None),
        P("section", None),
        P("section", None),
        P("section", "dp", None),
        P("section", "dp", None),
    )
    out_specs = (P("section", None, "dp", None), P("section", "dp", None))
    return jax.shard_map(
        per_device, mesh=mesh, in_specs=in_specs, out_specs=out_specs, check_vma=False
    )
```

```python
import functools

import jax
import jax.numpy as jnp
from jax import lax
from jax.experimental import pallas as pl
from jax.experimental.pallas import tpu as pltpu
from jax.sharding import PartitionSpec as P

epsilon = 1e-05
piece_rows = 8
ticks_per_hop = 2


def whole_kernel(right_ref, rows_ref, owner_ref, gain_ref, whole_ref):
    column_block = pl.program_id(1)
    spread = jnp.where(
        owner_ref[...] == column_block, rows_ref[...].astype(jnp.float32), 0.0
    ).astype(jnp.bfloat16)
    product = jnp.dot(right_ref[...], spread, preferred_element_type=jnp.float32)
    whole_ref[...] = (product * gain_ref[...]).astype(jnp.bfloat16)


def build_maps(gain_row, order, right_full, left_full):
    channels, block = left_full.shape
    count = channels // block
    inverse = jnp.zeros((channels,), jnp.int32).at[order].set(jnp.arange(channels, dtype=jnp.int32))
    rows = jnp.take(left_full, inverse, axis=0)
    whole = pl.pallas_call(
        whole_kernel,
        grid=(count, count),
        in_specs=[
            pl.BlockSpec((block, block), lambda n, b: (n, 0)),
            pl.BlockSpec((block, block), lambda n, b: (n, 0)),
            pl.BlockSpec((block, 1), lambda n, b: (n, 0)),
            pl.BlockSpec((block, 1), lambda n, b: (n, 0)),
        ],
        out_specs=pl.BlockSpec((block, block), lambda n, b: (n, b)),
        out_shape=jax.ShapeDtypeStruct((channels, channels), jnp.bfloat16),
        name="whole_map",
    )(right_full, rows, (inverse // block)[:, None], gain_row[:, None])
    pick = (order[None, :block] == jnp.arange(channels)[:, None]).astype(jnp.bfloat16)
    head = jnp.einsum(
        "nkj,nji->nki",
        right_full.reshape(count, block, block),
        pick.reshape(count, block, block),
        preferred_element_type=jnp.float32,
    ).astype(jnp.bfloat16).reshape(channels, block)
    return whole, head


def inverse_norm(wide_in):
    return lax.rsqrt(jnp.mean(wide_in * wide_in, axis=-1, keepdims=True) + epsilon)


def relay_kernel(
    sections, in_ref, grad_ref, whole_ref, out_ref, saved_ref, up_ref,
    held, upstream, sent, scaled, forward_send, forward_recv, backward_send, backward_recv,
):
    me = lax.axis_index("section")
    micro_count, row_count, channels = held.shape
    chunk = up_ref.shape[2]
    after = lax.rem(me + 1, sections)
    ahead = lax.rem(me + sections - 1, sections)

    barrier = pltpu.get_barrier_semaphore()
    for neighbour in (after, ahead):
        pl.semaphore_signal(
            barrier, inc=1, device_id={"section": neighbour}, device_id_type=pl.DeviceIdType.MESH
        )

    @pl.when(me == 0)
    def first_inputs():
        held[...] = in_ref[...]

    @pl.when(me == sections - 1)
    def last_grads():
        upstream[...] = grad_ref[...]

    pl.semaphore_wait(barrier, 2)

    def forward_copy(slot):
        return pltpu.make_async_remote_copy(
            src_ref=out_ref.at[slot],
            dst_ref=held.at[slot],
            send_sem=forward_send.at[slot],
            recv_sem=forward_recv.at[slot],
            device_id={"section": after},
            device_id_type=pl.DeviceIdType.MESH,
        )

    def backward_copy(slot):
        return pltpu.make_async_remote_copy(
            src_ref=sent.at[slot],
            dst_ref=upstream.at[slot],
            send_sem=backward_send.at[slot],
            recv_sem=backward_recv.at[slot],
            device_id={"section": ahead},
            device_id_type=pl.DeviceIdType.MESH,
        )

    def run_forward(slot):
        @pl.when(me > 0)
        def arrived():
            forward_copy(slot).wait_recv()

        wide = held[slot].astype(jnp.float32)
        inverse_rms = inverse_norm(wide)

        def columns(part, carry):
            cols = pl.ds(pl.multiple_of(part * chunk, chunk), chunk)
            product = jnp.dot(held[slot], whole_ref[:, cols], preferred_element_type=jnp.float32)
            out_ref[slot, :, cols] = (
                held[slot, :, cols].astype(jnp.float32) + inverse_rms * product
            ).astype(jnp.bfloat16)
            return carry

        lax.fori_loop(0, channels // chunk, columns, 0)

        @pl.when(me < sections - 1)
        def pass_on():
            forward_copy(slot).start()

    def run_backward(slot):
        @pl.when(me < sections - 1)
        def arrived():
            backward_copy(slot).wait_recv()

        @pl.when(me > 0)
        def compute():
            def columns(part, carry):
                cols = pl.ds(pl.multiple_of(part * chunk, chunk), chunk)
                scaled[:, cols] = lax.dot_general(
                    upstream[slot], whole_ref[cols, :], (((1,), (1,)), ((), ())),
                    preferred_element_type=jnp.float32,
                )
                return carry

            lax.fori_loop(0, channels // chunk, columns, 0)
            wide = held[slot].astype(jnp.float32)
            inverse_rms = inverse_norm(wide)
            terms = scaled[...]
            along = jnp.mean(terms * wide, axis=-1, keepdims=True)
            cubed = inverse_rms * inverse_rms * inverse_rms
            sent[slot] = (
                upstream[slot].astype(jnp.float32) + inverse_rms * terms - wide * (cubed * along)
            ).astype(jnp.bfloat16)
            backward_copy(slot).start()

    def tick(step, carry):
        forward_slot = step - ticks_per_hop * me
        backward_slot = step - ticks_per_hop * (2 * sections - 2 - me) - 1

        @pl.when((forward_slot >= 0) & (forward_slot < micro_count))
        def forward_part():
            run_forward(forward_slot)

        @pl.when((backward_slot >= 0) & (backward_slot < micro_count))
        def backward_part():
            run_backward(backward_slot)

        return carry

    lax.fori_loop(0, ticks_per_hop * (2 * sections - 2) + 1 + micro_count, tick, 0)
    saved_ref[...] = held[...]
    up_ref[...] = upstream[:, :, :chunk]

    @pl.when(me < sections - 1)
    def forward_sent():
        lax.fori_loop(0, micro_count, lambda slot, carry: (forward_copy(slot).wait_send(), carry)[1], 0)

    @pl.when(me > 0)
    def backward_sent():
        lax.fori_loop(0, micro_count, lambda slot, carry: (backward_copy(slot).wait_send(), carry)[1], 0)


def relay(sections, section_input, loss_grad, whole, block_size):
    shape = section_input.shape
    head_shape = shape[:2] + (block_size,)
    vmem = pl.BlockSpec(memory_space=pltpu.VMEM)
    sems = pltpu.SemaphoreType.DMA((shape[0],))
    return pl.pallas_call(
        functools.partial(relay_kernel, sections),
        out_shape=[
            jax.ShapeDtypeStruct(shape, jnp.bfloat16),
            jax.ShapeDtypeStruct(shape, jnp.bfloat16),
            jax.ShapeDtypeStruct(head_shape, jnp.bfloat16),
        ],
        in_specs=[vmem] * 3,
        out_specs=[vmem] * 3,
        scratch_shapes=[
            pltpu.VMEM(shape, jnp.bfloat16),
            pltpu.VMEM(shape, jnp.bfloat16),
            pltpu.VMEM(shape, jnp.bfloat16),
            pltpu.VMEM(shape[1:], jnp.float32),
            sems, sems, sems, sems,
        ],
        compiler_params=pltpu.CompilerParams(
            collective_id=0, has_side_effects=True, vmem_limit_bytes=48 * 1024 * 1024
        ),
        name="relay",
    )(section_input, loss_grad, whole)


def per_device(section_input, loss_grad, norm_gain, channel_order, right_factor, left_factor):
    sections = lax.axis_size("section")
    micro_count, row_count, channels = section_input.shape
    block_size = right_factor.shape[2]
    left_full = lax.all_gather(left_factor[0], "dp", axis=0, tiled=True)
    right_full = lax.all_gather(right_factor[0], "dp", axis=0, tiled=True)
    gain_row = norm_gain[0]
    whole, head = build_maps(gain_row, channel_order[0], right_full, left_full)
    pieces = (micro_count * row_count // piece_rows, piece_rows, channels)
    outputs, saved_in, saved_up = relay(
        sections, section_input.reshape(pieces), loss_grad.reshape(pieces), whole, block_size
    )

    row_total = micro_count * row_count
    wide_in = saved_in.reshape(row_total, channels).astype(jnp.float32)
    normed = (wide_in * inverse_norm(wide_in) * gain_row).astype(jnp.bfloat16)
    permuted = jnp.dot(normed, head, preferred_element_type=jnp.float32).astype(jnp.bfloat16)
    left_shard = left_gradient(permuted, saved_up.reshape(row_total, block_size))
    return (outputs.reshape(section_input.shape)[None], left_shard[None])


def left_gradient(left_rows, right_rows):
    peers = lax.axis_size("dp")
    block_size = left_rows.shape[1]
    term = lax.dot_general(
        left_rows, right_rows, (((0,), (0,)), ((), ())), preferred_element_type=jnp.float32
    ).astype(jnp.bfloat16)
    parts = lax.all_to_all(
        term.reshape(peers, block_size // peers, block_size), "dp", split_axis=0, concat_axis=0
    )
    return jnp.sum(parts.astype(jnp.float32), axis=0)


def solution(mesh):
    in_specs = (
        P(None, "dp", None),
        P(None, "dp", None),
        P("section", None),
        P("section", None),
        P("section", "dp", None),
        P("section", "dp", None),
    )
    out_specs = (P("section", None, "dp", None), P("section", "dp", None))
    return jax.shard_map(
        per_device, mesh=mesh, in_specs=in_specs, out_specs=out_specs, check_vma=False
    )
```

```python
import functools

import jax
import jax.numpy as jnp
from jax import lax
from jax.experimental import pallas as pl
from jax.experimental.pallas import tpu as pltpu
from jax.sharding import PartitionSpec as P

epsilon = 1e-05
piece_rows = 16
ticks_per_hop = 2


def whole_kernel(right_ref, rows_ref, owner_ref, gain_ref, whole_ref):
    column_block = pl.program_id(1)
    spread = jnp.where(
        owner_ref[...] == column_block, rows_ref[...].astype(jnp.float32), 0.0
    ).astype(jnp.bfloat16)
    product = jnp.dot(right_ref[...], spread, preferred_element_type=jnp.float32)
    whole_ref[...] = (product * gain_ref[...]).astype(jnp.bfloat16)


def build_maps(gain_row, order, right_full, left_full):
    channels, block = left_full.shape
    count = channels // block
    inverse = jnp.zeros((channels,), jnp.int32).at[order].set(jnp.arange(channels, dtype=jnp.int32))
    rows = jnp.take(left_full, inverse, axis=0)
    whole = pl.pallas_call(
        whole_kernel,
        grid=(count, count),
        in_specs=[
            pl.BlockSpec((block, block), lambda n, b: (n, 0)),
            pl.BlockSpec((block, block), lambda n, b: (n, 0)),
            pl.BlockSpec((block, 1), lambda n, b: (n, 0)),
            pl.BlockSpec((block, 1), lambda n, b: (n, 0)),
        ],
        out_specs=pl.BlockSpec((block, block), lambda n, b: (n, b)),
        out_shape=jax.ShapeDtypeStruct((channels, channels), jnp.bfloat16),
        name="whole_map",
    )(right_full, rows, (inverse // block)[:, None], gain_row[:, None])
    pick = (order[None, :block] == jnp.arange(channels)[:, None]).astype(jnp.bfloat16)
    head = jnp.einsum(
        "nkj,nji->nki",
        right_full.reshape(count, block, block),
        pick.reshape(count, block, block),
        preferred_element_type=jnp.float32,
    ).astype(jnp.bfloat16).reshape(channels, block)
    return whole, head


def inverse_norm(wide_in):
    return lax.rsqrt(jnp.mean(wide_in * wide_in, axis=-1, keepdims=True) + epsilon)


def relay_kernel(
    sections, in_ref, grad_ref, whole_ref, out_ref, saved_ref, up_ref,
    held, upstream, sent, scaled, forward_send, forward_recv, backward_send, backward_recv,
):
    me = lax.axis_index("section")
    micro_count, row_count, channels = held.shape
    chunk = up_ref.shape[2]
    after = lax.rem(me + 1, sections)
    ahead = lax.rem(me + sections - 1, sections)

    barrier = pltpu.get_barrier_semaphore()
    for neighbour in (after, ahead):
        pl.semaphore_signal(
            barrier, inc=1, device_id={"section": neighbour}, device_id_type=pl.DeviceIdType.MESH
        )

    @pl.when(me == 0)
    def first_inputs():
        held[...] = in_ref[...]

    @pl.when(me == sections - 1)
    def last_grads():
        upstream[...] = grad_ref[...]

    pl.semaphore_wait(barrier, 2)

    parts = channels // chunk

    def forward_copy(slot, part):
        cols = pl.ds(pl.multiple_of(part * chunk, chunk), chunk)
        return pltpu.make_async_remote_copy(
            src_ref=out_ref.at[slot, :, cols],
            dst_ref=held.at[slot, :, cols],
            send_sem=forward_send.at[slot, part],
            recv_sem=forward_recv.at[slot, part],
            device_id={"section": after},
            device_id_type=pl.DeviceIdType.MESH,
        )

    def backward_copy(slot):
        return pltpu.make_async_remote_copy(
            src_ref=sent.at[slot],
            dst_ref=upstream.at[slot],
            send_sem=backward_send.at[slot],
            recv_sem=backward_recv.at[slot],
            device_id={"section": ahead},
            device_id_type=pl.DeviceIdType.MESH,
        )

    def run_forward(slot):
        @pl.when(me > 0)
        def arrived():
            for part in range(parts):
                forward_copy(slot, part).wait_recv()

        wide = held[slot].astype(jnp.float32)
        inverse_rms = inverse_norm(wide)

        def columns(part, carry):
            cols = pl.ds(pl.multiple_of(part * chunk, chunk), chunk)
            product = jnp.dot(held[slot], whole_ref[:, cols], preferred_element_type=jnp.float32)
            out_ref[slot, :, cols] = (
                held[slot, :, cols].astype(jnp.float32) + inverse_rms * product
            ).astype(jnp.bfloat16)

            @pl.when(me < sections - 1)
            def pass_on():
                forward_copy(slot, part).start()

            return carry

        lax.fori_loop(0, parts, columns, 0)

    def run_backward(slot):
        @pl.when(me < sections - 1)
        def arrived():
            backward_copy(slot).wait_recv()

        @pl.when(me > 0)
        def compute():
            def columns(part, carry):
                cols = pl.ds(pl.multiple_of(part * chunk, chunk), chunk)
                scaled[:, cols] = lax.dot_general(
                    upstream[slot], whole_ref[cols, :], (((1,), (1,)), ((), ())),
                    preferred_element_type=jnp.float32,
                )
                return carry

            lax.fori_loop(0, parts, columns, 0)
            wide = held[slot].astype(jnp.float32)
            inverse_rms = inverse_norm(wide)
            terms = scaled[...]
            along = jnp.mean(terms * wide, axis=-1, keepdims=True)
            cubed = inverse_rms * inverse_rms * inverse_rms
            sent[slot] = (
                upstream[slot].astype(jnp.float32) + inverse_rms * terms - wide * (cubed * along)
            ).astype(jnp.bfloat16)
            backward_copy(slot).start()

    def tick(step, carry):
        forward_slot = step - ticks_per_hop * me
        backward_slot = step - ticks_per_hop * (2 * sections - 2 - me) - 1

        @pl.when((forward_slot >= 0) & (forward_slot < micro_count))
        def forward_part():
            run_forward(forward_slot)

        @pl.when((backward_slot >= 0) & (backward_slot < micro_count))
        def backward_part():
            run_backward(backward_slot)

        return carry

    lax.fori_loop(0, ticks_per_hop * (2 * sections - 2) + 1 + micro_count, tick, 0)
    saved_ref[...] = held[...]
    up_ref[...] = upstream[:, :, :chunk]

    @pl.when(me < sections - 1)
    def forward_sent():
        def sent_piece(slot, carry):
            for part in range(parts):
                forward_copy(slot, part).wait_send()
            return carry

        lax.fori_loop(0, micro_count, sent_piece, 0)

    @pl.when(me > 0)
    def backward_sent():
        lax.fori_loop(0, micro_count, lambda slot, carry: (backward_copy(slot).wait_send(), carry)[1], 0)


def relay(sections, section_input, loss_grad, whole, block_size):
    shape = section_input.shape
    head_shape = shape[:2] + (block_size,)
    vmem = pl.BlockSpec(memory_space=pltpu.VMEM)
    sems = pltpu.SemaphoreType.DMA((shape[0],))
    part_sems = pltpu.SemaphoreType.DMA((shape[0], shape[2] // block_size))
    return pl.pallas_call(
        functools.partial(relay_kernel, sections),
        out_shape=[
            jax.ShapeDtypeStruct(shape, jnp.bfloat16),
            jax.ShapeDtypeStruct(shape, jnp.bfloat16),
            jax.ShapeDtypeStruct(head_shape, jnp.bfloat16),
        ],
        in_specs=[vmem] * 3,
        out_specs=[vmem] * 3,
        scratch_shapes=[
            pltpu.VMEM(shape, jnp.bfloat16),
            pltpu.VMEM(shape, jnp.bfloat16),
            pltpu.VMEM(shape, jnp.bfloat16),
            pltpu.VMEM(shape[1:], jnp.float32),
            part_sems, part_sems, sems, sems,
        ],
        compiler_params=pltpu.CompilerParams(
            collective_id=0, has_side_effects=True, vmem_limit_bytes=48 * 1024 * 1024
        ),
        name="relay",
    )(section_input, loss_grad, whole)


def per_device(section_input, loss_grad, norm_gain, channel_order, right_factor, left_factor):
    sections = lax.axis_size("section")
    micro_count, row_count, channels = section_input.shape
    block_size = right_factor.shape[2]
    left_full = lax.all_gather(left_factor[0], "dp", axis=0, tiled=True)
    right_full = lax.all_gather(right_factor[0], "dp", axis=0, tiled=True)
    gain_row = norm_gain[0]
    whole, head = build_maps(gain_row, channel_order[0], right_full, left_full)
    pieces = (micro_count * row_count // piece_rows, piece_rows, channels)
    outputs, saved_in, saved_up = relay(
        sections, section_input.reshape(pieces), loss_grad.reshape(pieces), whole, block_size
    )

    row_total = micro_count * row_count
    wide_in = saved_in.reshape(row_total, channels).astype(jnp.float32)
    normed = (wide_in * inverse_norm(wide_in) * gain_row).astype(jnp.bfloat16)
    permuted = jnp.dot(normed, head, preferred_element_type=jnp.float32).astype(jnp.bfloat16)
    left_shard = left_gradient(permuted, saved_up.reshape(row_total, block_size))
    return (outputs.reshape(section_input.shape)[None], left_shard[None])


def left_gradient(left_rows, right_rows):
    peers = lax.axis_size("dp")
    block_size = left_rows.shape[1]
    term = lax.dot_general(
        left_rows, right_rows, (((0,), (0,)), ((), ())), preferred_element_type=jnp.float32
    ).astype(jnp.bfloat16)
    parts = lax.all_to_all(
        term.reshape(peers, block_size // peers, block_size), "dp", split_axis=0, concat_axis=0
    )
    return jnp.sum(parts.astype(jnp.float32), axis=0)


def solution(mesh):
    in_specs = (
        P(None, "dp", None),
        P(None, "dp", None),
        P("section", None),
        P("section", None),
        P("section", "dp", None),
        P("section", "dp", None),
    )
    out_specs = (P("section", None, "dp", None), P("section", "dp", None))
    return jax.shard_map(
        per_device, mesh=mesh, in_specs=in_specs, out_specs=out_specs, check_vma=False
    )
```

```python
import functools

import jax
import jax.numpy as jnp
from jax import lax
from jax.experimental import pallas as pl
from jax.experimental.pallas import tpu as pltpu
from jax.sharding import PartitionSpec as P

epsilon = 1e-05
piece_rows = 16
ticks_per_hop = 2


def whole_kernel(right_ref, rows_ref, owner_ref, gain_ref, whole_ref):
    column_block = pl.program_id(1)
    spread = jnp.where(
        owner_ref[...] == column_block, rows_ref[...].astype(jnp.float32), 0.0
    ).astype(jnp.bfloat16)
    product = jnp.dot(right_ref[...], spread, preferred_element_type=jnp.float32)
    whole_ref[...] = (product * gain_ref[...]).astype(jnp.bfloat16)


def build_maps(gain_row, order, right_full, left_full):
    channels, block = left_full.shape
    count = channels // block
    inverse = jnp.zeros((channels,), jnp.int32).at[order].set(jnp.arange(channels, dtype=jnp.int32))
    rows = jnp.take(left_full, inverse, axis=0)
    whole = pl.pallas_call(
        whole_kernel,
        grid=(count, count),
        in_specs=[
            pl.BlockSpec((block, block), lambda n, b: (n, 0)),
            pl.BlockSpec((block, block), lambda n, b: (n, 0)),
            pl.BlockSpec((block, 1), lambda n, b: (n, 0)),
            pl.BlockSpec((block, 1), lambda n, b: (n, 0)),
        ],
        out_specs=pl.BlockSpec((block, block), lambda n, b: (n, b)),
        out_shape=jax.ShapeDtypeStruct((channels, channels), jnp.bfloat16),
        name="whole_map",
    )(right_full, rows, (inverse // block)[:, None], gain_row[:, None])
    pick = (order[None, :block] == jnp.arange(channels)[:, None]).astype(jnp.bfloat16)
    head = jnp.einsum(
        "nkj,nji->nki",
        right_full.reshape(count, block, block),
        pick.reshape(count, block, block),
        preferred_element_type=jnp.float32,
    ).astype(jnp.bfloat16).reshape(channels, block)
    return whole, head


def inverse_norm(wide_in):
    return lax.rsqrt(jnp.mean(wide_in * wide_in, axis=-1, keepdims=True) + epsilon)


def relay_kernel(
    sections, in_ref, grad_ref, whole_ref, out_ref, saved_ref, up_ref,
    held, upstream, sent, scaled, forward_send, forward_recv, backward_send, backward_recv,
):
    me = lax.axis_index("section")
    micro_count, row_count, channels = held.shape
    chunk = up_ref.shape[2]
    after = lax.rem(me + 1, sections)
    ahead = lax.rem(me + sections - 1, sections)

    barrier = pltpu.get_barrier_semaphore()
    for neighbour in (after, ahead):
        pl.semaphore_signal(
            barrier, inc=1, device_id={"section": neighbour}, device_id_type=pl.DeviceIdType.MESH
        )

    @pl.when(me == 0)
    def first_inputs():
        held[...] = in_ref[...]

    @pl.when(me == sections - 1)
    def last_grads():
        upstream[...] = grad_ref[...]

    pl.semaphore_wait(barrier, 2)

    parts = channels // chunk

    def forward_copy(slot, part):
        cols = pl.ds(pl.multiple_of(part * chunk, chunk), chunk)
        return pltpu.make_async_remote_copy(
            src_ref=out_ref.at[slot, :, cols],
            dst_ref=held.at[slot, :, cols],
            send_sem=forward_send.at[slot, part],
            recv_sem=forward_recv.at[slot, part],
            device_id={"section": after},
            device_id_type=pl.DeviceIdType.MESH,
        )

    def backward_copy(slot):
        return pltpu.make_async_remote_copy(
            src_ref=sent.at[slot],
            dst_ref=upstream.at[slot],
            send_sem=backward_send.at[slot],
            recv_sem=backward_recv.at[slot],
            device_id={"section": ahead},
            device_id_type=pl.DeviceIdType.MESH,
        )

    def run_forward(slot):
        @pl.when(me > 0)
        def arrived():
            for part in range(parts):
                forward_copy(slot, part).wait_recv()

        wide = held[slot].astype(jnp.float32)
        inverse_rms = inverse_norm(wide)

        def columns(part, carry):
            cols = pl.ds(pl.multiple_of(part * chunk, chunk), chunk)
            product = jnp.dot(held[slot], whole_ref[:, cols], preferred_element_type=jnp.float32)
            out_ref[slot, :, cols] = (
                held[slot, :, cols].astype(jnp.float32) + inverse_rms * product
            ).astype(jnp.bfloat16)

            @pl.when(me < sections - 1)
            def pass_on():
                forward_copy(slot, part).start()

            return carry

        lax.fori_loop(0, parts, columns, 0)

    def back_product(slot):
        def columns(part, carry):
            cols = pl.ds(pl.multiple_of(part * chunk, chunk), chunk)
            scaled[slot, :, cols] = lax.dot_general(
                upstream[slot], whole_ref[cols, :], (((1,), (1,)), ((), ())),
                preferred_element_type=jnp.float32,
            )
            return carry

        lax.fori_loop(0, parts, columns, 0)

    def run_backward(slot):
        @pl.when(me < sections - 1)
        def arrived():
            backward_copy(slot).wait_recv()

        @pl.when((me > 0) & (me < sections - 1))
        def product():
            back_product(slot)

        @pl.when(me > 0)
        def compute():
            wide = held[slot].astype(jnp.float32)
            inverse_rms = inverse_norm(wide)
            terms = scaled[slot]
            along = jnp.mean(terms * wide, axis=-1, keepdims=True)
            cubed = inverse_rms * inverse_rms * inverse_rms
            sent[slot] = (
                upstream[slot].astype(jnp.float32) + inverse_rms * terms - wide * (cubed * along)
            ).astype(jnp.bfloat16)
            backward_copy(slot).start()

    @pl.when(me == sections - 1)
    def products_ahead():
        lax.fori_loop(0, micro_count, lambda slot, carry: (back_product(slot), carry)[1], 0)

    def tick(step, carry):
        forward_slot = step - ticks_per_hop * me
        backward_slot = step - ticks_per_hop * (2 * sections - 2 - me) - 1

        @pl.when((forward_slot >= 0) & (forward_slot < micro_count))
        def forward_part():
            run_forward(forward_slot)

        @pl.when((backward_slot >= 0) & (backward_slot < micro_count))
        def backward_part():
            run_backward(backward_slot)

        return carry

    lax.fori_loop(0, ticks_per_hop * (2 * sections - 2) + 1 + micro_count, tick, 0)
    saved_ref[...] = held[...]
    up_ref[...] = upstream[:, :, :chunk]

    @pl.when(me < sections - 1)
    def forward_sent():
        def sent_piece(slot, carry):
            for part in range(parts):
                forward_copy(slot, part).wait_send()
            return carry

        lax.fori_loop(0, micro_count, sent_piece, 0)

    @pl.when(me > 0)
    def backward_sent():
        lax.fori_loop(0, micro_count, lambda slot, carry: (backward_copy(slot).wait_send(), carry)[1], 0)


def relay(sections, section_input, loss_grad, whole, block_size):
    shape = section_input.shape
    head_shape = shape[:2] + (block_size,)
    vmem = pl.BlockSpec(memory_space=pltpu.VMEM)
    sems = pltpu.SemaphoreType.DMA((shape[0],))
    part_sems = pltpu.SemaphoreType.DMA((shape[0], shape[2] // block_size))
    return pl.pallas_call(
        functools.partial(relay_kernel, sections),
        out_shape=[
            jax.ShapeDtypeStruct(shape, jnp.bfloat16),
            jax.ShapeDtypeStruct(shape, jnp.bfloat16),
            jax.ShapeDtypeStruct(head_shape, jnp.bfloat16),
        ],
        in_specs=[vmem] * 3,
        out_specs=[vmem] * 3,
        scratch_shapes=[
            pltpu.VMEM(shape, jnp.bfloat16),
            pltpu.VMEM(shape, jnp.bfloat16),
            pltpu.VMEM(shape, jnp.bfloat16),
            pltpu.VMEM(shape, jnp.float32),
            part_sems, part_sems, sems, sems,
        ],
        compiler_params=pltpu.CompilerParams(
            collective_id=0, has_side_effects=True, vmem_limit_bytes=48 * 1024 * 1024
        ),
        name="relay",
    )(section_input, loss_grad, whole)


def per_device(section_input, loss_grad, norm_gain, channel_order, right_factor, left_factor):
    sections = lax.axis_size("section")
    micro_count, row_count, channels = section_input.shape
    block_size = right_factor.shape[2]
    left_full = lax.all_gather(left_factor[0], "dp", axis=0, tiled=True)
    right_full = lax.all_gather(right_factor[0], "dp", axis=0, tiled=True)
    gain_row = norm_gain[0]
    whole, head = build_maps(gain_row, channel_order[0], right_full, left_full)
    pieces = (micro_count * row_count // piece_rows, piece_rows, channels)
    outputs, saved_in, saved_up = relay(
        sections, section_input.reshape(pieces), loss_grad.reshape(pieces), whole, block_size
    )

    row_total = micro_count * row_count
    wide_in = saved_in.reshape(row_total, channels).astype(jnp.float32)
    normed = (wide_in * inverse_norm(wide_in) * gain_row).astype(jnp.bfloat16)
    permuted = jnp.dot(normed, head, preferred_element_type=jnp.float32).astype(jnp.bfloat16)
    left_shard = left_gradient(permuted, saved_up.reshape(row_total, block_size))
    return (outputs.reshape(section_input.shape)[None], left_shard[None])


def left_gradient(left_rows, right_rows):
    peers = lax.axis_size("dp")
    block_size = left_rows.shape[1]
    term = lax.dot_general(
        left_rows, right_rows, (((0,), (0,)), ((), ())), preferred_element_type=jnp.float32
    ).astype(jnp.bfloat16)
    parts = lax.all_to_all(
        term.reshape(peers, block_size // peers, block_size), "dp", split_axis=0, concat_axis=0
    )
    return jnp.sum(parts.astype(jnp.float32), axis=0)


def solution(mesh):
    in_specs = (
        P(None, "dp", None),
        P(None, "dp", None),
        P("section", None),
        P("section", None),
        P("section", "dp", None),
        P("section", "dp", None),
    )
    out_specs = (P("section", None, "dp", None), P("section", "dp", None))
    return jax.shard_map(
        per_device, mesh=mesh, in_specs=in_specs, out_specs=out_specs, check_vma=False
    )
```
